256 devices in a mesh: src: 32 (over z, y_hi, core), tgt: 8 (over y_lo, x).
Axes of the slice: x: 4, y: 4 (y_hi: 2, y_lo: 2; y = y_hi * 2 + y_lo), z: 8, core: 2. Of those that a mesh axis runs over, the one named last changes fastest.
Arguments:
- src_emb: bfloat16 [16384, 1024], P('src', 'tgt'), may hold values from -16 to 16
- tgt_emb: bfloat16 [32768, 1024], P('tgt', 'src'), may hold values from -16 to 16
- src_ids: int32 [16384], P('src'), may hold values from 0 to 16383
- tgt_ids: int32 [32768], P('tgt'), may hold values from 0 to 16383
Outputs:
- margin: float32 [16384, 32768], P('src', 'tgt')
The draws below stay inside these ranges and needn't reach their ends.
All inputs are finite; a program needn't handle non-finite values.
Results may differ from the reference program's by a relative error of at most 0.004.
Values may be sent and summed in bfloat16 or wider, within the bound.
No kernel may reach another device: no remote copies, remote signals or barrier semaphores. Data moves between devices by JAX's collectives and lax.ppermute only.
A program may use at most 64 MiB of HBM per device.

```python
import jax
import jax.numpy as jnp
from jax import lax

D = 1024
NEIGH = 4
NS = 16384
NT = 32768


def sentence_tables(key):
    group_rows = jax.random.normal(jax.random.fold_in(key, 11), (NT // 4, D), jnp.float32)
    ident_rows = jax.random.normal(jax.random.fold_in(key, 12), (NT // 2, D), jnp.float32)
    shared_part = jax.random.uniform(jax.random.fold_in(key, 13), (NT // 4,), jnp.float32, 0.1, 0.5)
    own_part = jax.random.uniform(jax.random.fold_in(key, 14), (NT // 2,), jnp.float32, 0.2, 0.45)
    return (group_rows, ident_rows, shared_part, own_part)


def draw_src_ids(key, part):
    return jax.random.randint(jax.random.fold_in(key, 21), (NS,), 0, NT // 2, dtype=jnp.int32)


def draw_tgt_ids(key, part):
    return jax.random.randint(jax.random.fold_in(key, 22), (NT,), 0, NT // 2, dtype=jnp.int32)


def mixed_rows(key, sentence_ids, salt):
    group_rows, ident_rows, shared_part, own_part = sentence_tables(key)
    count = sentence_ids.shape[0]
    group_ids = sentence_ids // 2
    shared_weight = jnp.take(shared_part, group_ids)
    own_weight = jnp.take(own_part, sentence_ids)
    rest_weight = 1.0 - shared_weight - own_weight
    noise_key = jax.random.fold_in(key, salt)
    noise = jax.random.normal(noise_key, (count, D), jnp.float32)
    rows = jnp.sqrt(shared_weight)[:, None] * jnp.take(group_rows, group_ids, axis=0)
    rows = rows + jnp.sqrt(own_weight)[:, None] * jnp.take(ident_rows, sentence_ids, axis=0)
    rows = rows + jnp.sqrt(rest_weight)[:, None] * noise
    return jnp.clip(rows, -16.0, 16.0).astype(jnp.bfloat16)


def draw_src_emb(key, part):
    return mixed_rows(key, draw_src_ids(key, part), 31)


def draw_tgt_emb(key, part):
    return mixed_rows(key, draw_tgt_ids(key, part), 32)


def setup_inputs(seed: int = 0) -> dict:
    keys = jax.random.split(jax.random.key(seed), 5)
    src_emb = draw_src_emb(jax.random.fold_in(keys[4], 71), 0)
    tgt_emb = draw_tgt_emb(jax.random.fold_in(keys[4], 71), 0)
    src_ids = draw_src_ids(jax.random.fold_in(keys[4], 71), 0)
    tgt_ids = draw_tgt_ids(jax.random.fold_in(keys[4], 71), 0)
    return dict(src_emb=src_emb, tgt_emb=tgt_emb, src_ids=src_ids, tgt_ids=tgt_ids)


epsilon = 1e-06
excluded_score = -2.0

def unit_rows(embedded):
    values = embedded.astype(jnp.float32)
    scale = jnp.sqrt(lax.optimization_barrier(jnp.sum(values * values, axis=1, keepdims=True)) + epsilon)
    return (values / scale).astype(jnp.bfloat16)

def best_four(values):
    return lax.top_k(values, NEIGH)[0]

def reference(src_emb, tgt_emb, src_ids, tgt_ids):
    src_unit = unit_rows(src_emb)
    tgt_unit = unit_rows(tgt_emb)
    block_rows = min(512, NS)
    blocks = NS // block_rows
    src_blocks = src_unit.reshape(blocks, block_rows, D)
    id_blocks = src_ids.reshape(blocks, block_rows)

    def cosines(rows, row_ids):
        scores = lax.dot_general(rows, tgt_unit, (((1,), (1,)), ((), ())), preferred_element_type=jnp.float32)
        same = row_ids[:, None] == tgt_ids[None, :]
        return (jnp.where(same, jnp.float32(excluded_score), scores), same)

    def first_pass(column_best, pieces):
        rows, row_ids = pieces
        scores, same = cosines(rows, row_ids)
        row_best = best_four(scores)
        merged = best_four(jnp.concatenate([column_best, best_four(scores.T)], axis=1))
        return (merged, row_best)
    start = jnp.full((NT, NEIGH), excluded_score, jnp.float32)
    column_best, row_best = lax.scan(first_pass, start, (src_blocks, id_blocks))
    knn_src = lax.optimization_barrier(jnp.mean(row_best, axis=-1))
    knn_tgt = lax.optimization_barrier(jnp.mean(column_best, axis=-1))

    def second_pass(pieces):
        rows, row_ids, row_knn = pieces
        scores, same = cosines(rows, row_ids)
        ratio = scores / (0.5 * (row_knn[:, None] + knn_tgt[None, :]))
        return jnp.where(same, jnp.float32(0.0), ratio)
    margin = lax.map(second_pass, (src_blocks, id_blocks, knn_src))
    return margin.reshape(NS, NT)
```

```python
import functools

import jax
import jax.numpy as jnp
from jax import lax
from jax.experimental import pallas as pl
from jax.experimental.pallas import tpu as pltpu
from jax.sharding import Mesh
from jax.sharding import PartitionSpec as P

SRC = ("z", "yh", "core")
TGT = ("yl", "x")
EPS = 1e-06
EXCLUDED = -2.0


def bitonic_sorted(m):
    a, b, c, d = m
    a, c = jnp.maximum(a, c), jnp.minimum(a, c)
    b, d = jnp.maximum(b, d), jnp.minimum(b, d)
    a, b = jnp.maximum(a, b), jnp.minimum(a, b)
    c, d = jnp.maximum(c, d), jnp.minimum(c, d)
    return (a, b, c, d)


def top_half(first, second):
    return tuple(jnp.maximum(first[i], second[3 - i]) for i in range(4))


def merged(first, second):
    return bitonic_sorted(top_half(first, second))


def sorted_four(a, b, c, d):
    a, b = jnp.maximum(a, b), jnp.minimum(a, b)
    c, d = jnp.maximum(c, d), jnp.minimum(c, d)
    a, c = jnp.maximum(a, c), jnp.minimum(a, c)
    b, d = jnp.maximum(b, d), jnp.minimum(b, d)
    b, c = jnp.maximum(b, c), jnp.minimum(b, c)
    return (a, b, c, d)


def merged_all(lists):
    while len(lists) > 1:
        lists = [
            merged(lists[k], lists[k + 1]) if k + 1 < len(lists) else lists[k]
            for k in range(0, len(lists), 2)
        ]
    return lists[0]


def over_sublanes(lists):
    for shift in (4, 2, 1):
        lists = merged(lists, tuple(pltpu.roll(p, shift, 0) for p in lists))
    return lists


def score_kernel(
    n_blocks, places, tile, *refs
):
    blocks = refs[:n_blocks]
    src_ref, sid_ref, tid_ref = refs[n_blocks : n_blocks + 3]
    out_ref, row_ref, col_ref = refs[n_blocks + 3 : n_blocks + 6]
    tall, sraw, sunit, dots, rows, tsem, ssem = refs[n_blocks + 6 :]
    step = pl.program_id(0)
    steps = pl.num_programs(0)
    rows_n, feats = sunit.shape
    width = tall.shape[1]
    n_tiles = width // tile
    z = lax.axis_index("z")
    yh = lax.axis_index("yh")
    core = lax.axis_index("core")

    def copies():
        found = []
        for block, where in zip(blocks, places):
            for k, (dz, dy, dc) in enumerate(where):
                owner = (
                    lax.rem(z + 8 + dz, 8) * 4
                    + lax.rem(yh + dy, 2) * 2
                    + lax.rem(core + dc, 2)
                )
                piece = block.at[k] if len(block.shape) == 3 else block
                found.append((piece, pl.multiple_of(owner * 32, 32)))
        return found

    def copy(piece, start, n, tile_index):
        cols = pl.ds(pl.multiple_of(tile_index * tile, tile), tile)
        return pltpu.make_async_copy(
            piece.at[:, cols], tall.at[pl.ds(start, 32), cols], tsem.at[tile_index, n]
        )

    def src_copy(j):
        return pltpu.make_async_copy(
            src_ref.at[j], sraw.at[:, pl.ds(128 * j, 128)], ssem.at[j]
        )

    @pl.when(step == 0)
    def _():
        for j in range(8):
            src_copy(j).start()
        for t in range(n_tiles):
            for n, (piece, start) in enumerate(copies()):
                copy(piece, start, n, t).start()
        for j in range(8):
            src_copy(j).wait()
        for r in range(0, rows_n, 64):
            x = sraw[r : r + 64, :].astype(jnp.float32)
            scale = jnp.sqrt(jnp.sum(x * x, axis=1, keepdims=True) + EPS)
            sunit[r : r + 64, :] = (x / scale).astype(jnp.bfloat16)
        rows[...] = jnp.full(rows.shape, EXCLUDED, jnp.float32)

    for n, (piece, start) in enumerate(copies()):
        copy(piece, start, n, step).wait()

    cols = pl.ds(pl.multiple_of(step * tile, tile), tile)
    square = jnp.zeros((8, tile), jnp.float32)
    for k in range(0, feats, 64):
        x = tall[k : k + 64, cols].astype(jnp.float32)
        x = x * x
        for i in range(0, 64, 8):
            square = square + x[i : i + 8, :]
    inverse = 1.0 / jnp.sqrt(jnp.sum(square, axis=0, keepdims=True) + EPS)
    dots[...] = jnp.dot(sunit[...], tall[:, cols], preferred_element_type=jnp.float32)
    tid = tid_ref[...]
    groups = tile // 128

    def sweep(g, best):
        r = pl.multiple_of(g * 32, 32)
        pieces = []
        for k in range(4):
            here = pl.ds(r + 8 * k, 8)
            same = sid_ref[here, :] == tid
            x = jnp.where(same, jnp.float32(EXCLUDED), dots[here, :] * inverse)
            out_ref[here, :] = x
            pieces.append(x)
            for q in range(0, groups, 4):
                four = sorted_four(*(x[:, 128 * i : 128 * i + 128] for i in range(q, q + 4)))
                kept = merged(tuple(rows[i, here, :] for i in range(4)), four)
                for i in range(4):
                    rows[i, here, :] = kept[i]
        return merged(best, sorted_four(*pieces))

    empty = jnp.full((8, tile), EXCLUDED, jnp.float32)
    best = lax.fori_loop(0, rows_n // 32, sweep, (empty,) * 4)
    best = over_sublanes(best)
    for i in range(4):
        col_ref[i : i + 1, :] = best[i][0:1, :]

    @pl.when(step == steps - 1)
    def _():
        for r in range(0, rows_n, 128):
            turned = [rows[i, r : r + 128, :].T for i in range(4)]
            lists = [
                tuple(turned[i][q : q + 8, :] for i in range(4)) for q in range(0, 128, 8)
            ]
            final = over_sublanes(merged_all(lists))
            for i in range(4):
                row_ref[i : i + 1, r : r + 128] = final[i][0:1, :]


def scores_and_lists(blocks, places, src_all, sid, tid):
    tile = 512
    width = blocks[0].shape[-1]
    rows_n = src_all.shape[1]
    feats = 1024
    n_copies = sum(len(w) for w in places)
    any_spec = pl.BlockSpec(memory_space=pl.ANY)
    return pl.pallas_call(
        functools.partial(score_kernel, len(blocks), places, tile),
        grid=(width // tile,),
        out_shape=(
            jax.ShapeDtypeStruct((rows_n, width), jnp.float32),
            jax.ShapeDtypeStruct((4, rows_n), jnp.float32),
            jax.ShapeDtypeStruct((4, width), jnp.float32),
        ),
        in_specs=[any_spec] * len(blocks)
        + [
            any_spec,
            pl.BlockSpec((rows_n, 1), lambda i: (0, 0)),
            pl.BlockSpec((1, tile), lambda i: (0, i)),
        ],
        out_specs=(
            pl.BlockSpec((rows_n, tile), lambda i: (0, i)),
            pl.BlockSpec((4, rows_n), lambda i: (0, 0)),
            pl.BlockSpec((4, tile), lambda i: (0, i)),
        ),
        scratch_shapes=[
            pltpu.VMEM((feats, width), jnp.bfloat16),
            pltpu.VMEM((rows_n, feats), jnp.bfloat16),
            pltpu.VMEM((rows_n, feats), jnp.bfloat16),
            pltpu.VMEM((rows_n, tile), jnp.float32),
            pltpu.VMEM((4, rows_n, 128), jnp.float32),
            pltpu.SemaphoreType.DMA((width // tile, n_copies)),
            pltpu.SemaphoreType.DMA((8,)),
        ],
        compiler_params=pltpu.CompilerParams(
            dimension_semantics=("arbitrary",), vmem_limit_bytes=32 << 20
        ),
        cost_estimate=pl.CostEstimate(
            flops=2 * rows_n * width * feats, bytes_accessed=18 << 20, transcendentals=0
        ),
        name="scores",
    )(*blocks, src_all, sid, tid)


def margin_kernel(scores_ref, row_ref, knn_ref, out_ref, ksrc):
    @pl.when(pl.program_id(0) == 0)
    def _():
        lists = [tuple(row_ref[k, i : i + 1, :] for i in range(4)) for k in range(8)]
        a, b, c, d = merged_all(lists)
        mean = 0.25 * ((a + b) + (c + d))
        ksrc[...] = jnp.broadcast_to(mean, (128, mean.shape[1])).T

    rows_n = out_ref.shape[0]
    start = pl.multiple_of(pl.program_id(0) * rows_n, rows_n)
    knn_tgt = knn_ref[...]

    for r in range(0, rows_n, 8):
        knn_src = ksrc[pl.ds(start + r, 8), 0:1]
        x = scores_ref[r : r + 8, :]
        ratio = x / (0.5 * (knn_src + knn_tgt))
        out_ref[r : r + 8, :] = jnp.where(x < -1.5, jnp.float32(0.0), ratio)


def margin(scores, row_lists, knn_tgt):
    rows_n, width = scores.shape
    block = 64
    return pl.pallas_call(
        margin_kernel,
        grid=(rows_n // block,),
        out_shape=jax.ShapeDtypeStruct((rows_n, width), jnp.float32),
        in_specs=[
            pl.BlockSpec((block, width), lambda i: (i, 0)),
            pl.BlockSpec(row_lists.shape, lambda i: (0, 0, 0)),
            pl.BlockSpec((1, width), lambda i: (0, 0)),
        ],
        out_specs=pl.BlockSpec((block, width), lambda i: (i, 0)),
        scratch_shapes=[pltpu.VMEM((rows_n, 128), jnp.float32)],
        compiler_params=pltpu.CompilerParams(
            dimension_semantics=("arbitrary",), vmem_limit_bytes=24 << 20
        ),
        name="margin",
    )(scores, row_lists, knn_tgt)


def shifted(array, axis, size, by):
    return lax.ppermute(array, axis, [(i, (i + by) % size) for i in range(size)])


def from_everyone(array, axes, size):
    spread = jnp.broadcast_to(array[None], (size, *array.shape))
    return lax.all_to_all(spread, axes, 0, 0, tiled=True)


def body(src_emb, tgt_emb, src_ids, tgt_ids):
    src_all = lax.all_gather(src_emb, TGT, axis=0)
    own = tgt_emb.T
    up = lambda a: shifted(a, "z", 8, 1)
    down = lambda a: shifted(a, "z", 8, 7)
    over = lambda a: shifted(a, "core", 2, 1)
    other = shifted(own, "yh", 2, 1)
    rings = {}
    held = {("a", 1): own, ("a", -1): own, ("b", 1): other, ("b", -1): other}
    rings[(0, 0)] = own
    rings[(0, 1)] = other
    for step in range(1, 5):
        for name, dy in (("a", 0), ("b", 1)):
            for way in (1, -1):
                if step == 4 and way != (1 if name == "a" else -1):
                    continue
                held[name, way] = (up if way == 1 else down)(held[name, way])
                rings[(-step * way, dy)] = held[name, way]
    order = [
        [(0, 0), (0, 1), (-1, 0), (1, 0)],
        [(-1, 1), (1, 1), (-2, 0), (2, 0)],
        [(-2, 1), (2, 1), (-3, 0), (3, 0)],
        [(-3, 1), (3, 1), (-4, 0), (4, 1)],
    ]
    blocks, places = [], []
    for group in order:
        for key in group:
            blocks.append(rings[key])
            places.append(((*key, 0),))
        blocks.append(over(jnp.stack([rings[key] for key in group])))
        places.append(tuple((*key, 1) for key in group))

    scores, row_best, col_best = scores_and_lists(
        blocks, tuple(places), src_all, src_ids[:, None], tgt_ids[None, :]
    )
    row_lists = from_everyone(row_best, TGT, 8)
    col_best = col_best.astype(jnp.bfloat16)
    pair = over(col_best)
    half = col_best.shape[1] // 2
    start = lax.axis_index("core") * half
    mine, theirs = (
        lax.dynamic_slice_in_dim(a, start, half, 1).astype(jnp.float32)
        for a in (col_best, pair)
    )
    both = jnp.stack(merged(tuple(mine), tuple(theirs))).astype(jnp.bfloat16)
    col_lists = from_everyone(both, ("z", "yh"), 16).astype(jnp.float32)
    lists = [tuple(col_lists[k]) for k in range(16)]
    a, b, c, d = merged_all(lists)
    knn_half = 0.25 * ((a + b) + (c + d))
    knn_other = over(knn_half)
    first = lax.axis_index("core") == 0
    knn_tgt = jnp.concatenate(
        [jnp.where(first, knn_half, knn_other), jnp.where(first, knn_other, knn_half)]
    )
    return margin(scores, row_lists, knn_tgt[None, :])


def solution(mesh):
    finer = Mesh(mesh.devices.reshape(8, 2, 2, 2, 4), ("z", "yh", "core", "yl", "x"))
    in_specs = (P(SRC, TGT), P(TGT, SRC), P(SRC), P(TGT))
    return jax.shard_map(
        body, mesh=finer, in_specs=in_specs, out_specs=P(SRC, TGT), check_vma=False
    )
```

```python
import functools

import jax
import jax.numpy as jnp
from jax import lax
from jax.experimental import pallas as pl
from jax.experimental.pallas import tpu as pltpu
from jax.sharding import Mesh
from jax.sharding import PartitionSpec as P

SRC = ("z", "yh", "core")
TGT = ("yl", "x")
EPS = 1e-06
EXCLUDED = -2.0


def bitonic_sorted(m):
    a, b, c, d = m
    a, c = jnp.maximum(a, c), jnp.minimum(a, c)
    b, d = jnp.maximum(b, d), jnp.minimum(b, d)
    a, b = jnp.maximum(a, b), jnp.minimum(a, b)
    c, d = jnp.maximum(c, d), jnp.minimum(c, d)
    return (a, b, c, d)


def top_half(first, second):
    return tuple(jnp.maximum(first[i], second[3 - i]) for i in range(4))


def merged(first, second):
    return bitonic_sorted(top_half(first, second))


def sorted_four(a, b, c, d):
    a, b = jnp.maximum(a, b), jnp.minimum(a, b)
    c, d = jnp.maximum(c, d), jnp.minimum(c, d)
    a, c = jnp.maximum(a, c), jnp.minimum(a, c)
    b, d = jnp.maximum(b, d), jnp.minimum(b, d)
    b, c = jnp.maximum(b, c), jnp.minimum(b, c)
    return (a, b, c, d)


def merged_all(lists):
    while len(lists) > 1:
        lists = [
            merged(lists[k], lists[k + 1]) if k + 1 < len(lists) else lists[k]
            for k in range(0, len(lists), 2)
        ]
    return lists[0]


def over_sublanes(lists):
    for shift in (4, 2, 1):
        lists = merged(lists, tuple(pltpu.roll(p, shift, 0) for p in lists))
    return lists


def score_kernel(n_blocks, side, *refs):
    blocks = refs[:n_blocks]
    unit_refs = refs[n_blocks : n_blocks + 2]
    sid_ref, tid_ref = refs[n_blocks + 2 : n_blocks + 4]
    refs = refs[n_blocks + 4 :]
    if side:
        row_before, refs = refs[:2], refs[2:]
    score_refs, row_refs, col_ref = refs[:2], refs[2:4], refs[4]
    tall, unit, even, odd, rows, sids, stage, tsem, usem, osem = refs[5:]
    feats, width = tall.shape
    rows_n = unit.shape[0]
    half = rows_n // 2
    chunk, tile = even.shape
    n_units = width // tile
    z = lax.axis_index("z")
    yh = lax.axis_index("yh")

    def copy(n, t):
        dz, dy = PLACES[n]
        owner = lax.rem(z + (8 + dz), 8) * 2 + lax.rem(yh + dy, 2)
        where = pl.ds(pl.multiple_of(owner * 64, 64), 64)
        offset = side * width if blocks[n].shape[1] > width else 0
        return pltpu.make_async_copy(
            blocks[n].at[:, pl.ds(offset + t * tile, tile)],
            tall.at[where, pl.ds(t * tile, tile)],
            tsem.at[t, n],
        )

    unit_copies = [
        pltpu.make_async_copy(
            unit_refs[k], unit.at[pl.ds(k * half, half), :], usem.at[k]
        )
        for k in range(2)
    ]
    for n in range(n_blocks):
        copy(n, 0).start()
    for c in unit_copies:
        c.start()
    for t in range(1, n_units):
        for n in range(n_blocks):
            copy(n, t).start()
    for r in range(0, rows_n, 128):
        ids = jnp.broadcast_to(sid_ref[:, r : r + 128], (128, 128))
        sids[r : r + 128, :] = ids.T
    for r in range(0, rows_n, 32):
        for i in range(4):
            rows[i, r : r + 32, :] = jnp.full((32, 128), EXCLUDED, jnp.float32)

    def columns(u):
        return slice(u * tile, u * tile + tile)

    def inverse_norm(u):
        total = jnp.zeros((8, tile), jnp.float32)
        for k in range(0, feats, 16):
            x = tall[k : k + 16, columns(u)].astype(jnp.float32)
            x = x * x
            total = total + (x[:8] + x[8:])
        return 1.0 / jnp.sqrt(jnp.sum(total, axis=0, keepdims=True) + EPS)

    sequence = [(u, r) for u in range(n_units) for r in range(0, rows_n, chunk)]
    buffers = (even, odd)

    def dot(k):
        u, r = sequence[k]
        buffers[k % 2][...] = jnp.dot(
            unit[r : r + chunk, :],
            tall[:, columns(u)],
            preferred_element_type=jnp.float32,
        )

    def sweep(u, r, dots, inside, inverse, tid, best):
        pieces = []
        for k in range(0, 32, 8):
            here = slice(r + k, r + k + 8)
            ids = sids[here, :]
            same = jnp.concatenate([ids] * (tile // 128), axis=1) == tid
            dotted = dots[inside + k : inside + k + 8, :] * inverse
            x = jnp.where(same, jnp.float32(EXCLUDED), dotted)
            stage[here, columns(u)] = x
            pieces.append(x)
            kept = tuple(rows[i, here, :] for i in range(4))
            four = sorted_four(*(x[:, p : p + 128] for p in range(0, tile, 128)))
            kept = merged(kept, four)
            for i in range(4):
                rows[i, here, :] = kept[i]
        return merged(best, sorted_four(*pieces))

    def out_copy(k):
        u, r = sequence[k]
        cols = pl.ds(u * tile, tile)
        return pltpu.make_async_copy(
            stage.at[pl.ds(r, chunk), cols],
            score_refs[r // half].at[pl.ds(r % half, chunk), cols],
            osem.at[k],
        )

    for n in range(n_blocks):
        copy(n, 0).wait()
    for c in unit_copies:
        c.wait()
    dot(0)
    inverse = inverse_norm(0)
    best = (jnp.full((8, tile), EXCLUDED, jnp.float32),) * 4
    first = best
    for k, (u, r) in enumerate(sequence):
        if k + 1 < len(sequence):
            if sequence[k + 1][0] > u:
                for n in range(n_blocks):
                    copy(n, u + 1).wait()
                following = inverse_norm(u + 1)
            dot(k + 1)
        tid = tid_ref[:, columns(u)]
        for q in range(0, chunk, 32):
            best = sweep(u, r + q, buffers[k % 2], q, inverse, tid, best)
        out_copy(k).start()
        if r + chunk == rows_n:
            best = over_sublanes(best)
            for i in range(4):
                col_ref[i : i + 1, columns(u)] = best[i][0:1, :].astype(col_ref.dtype)
            if u + 1 < n_units:
                best, inverse = first, following

    for r in range(0, rows_n, 128):
        turned = [rows[i, r : r + 128, :].T for i in range(4)]
        lists = [
            tuple(turned[i][q : q + 8, :] for i in range(4)) for q in range(0, 128, 8)
        ]
        final = tuple(p[0:1, :] for p in over_sublanes(merged_all(lists)))
        here = slice(r % half, r % half + 128)
        if side:
            before = row_before[r // half]
            final = merged(final, tuple(before[i : i + 1, here] for i in range(4)))
        for i in range(4):
            row_refs[r // half][i : i + 1, here] = final[i]
    for k in range(len(sequence)):
        out_copy(k).wait()


def scores_and_lists(side, blocks, units, sid, tid, row_before):
    tile, chunk = 512, 256
    feats = 1024
    width = tid.shape[1]
    half = units[0].shape[0]
    vmem = pl.BlockSpec(memory_space=pltpu.VMEM)
    hbm = pl.BlockSpec(memory_space=pltpu.HBM)
    rest = [sid, tid, *row_before]
    return pl.pallas_call(
        functools.partial(score_kernel, len(blocks), side),
        out_shape=(
            pltpu.HBM((half, width), jnp.float32),
            pltpu.HBM((half, width), jnp.float32),
            jax.ShapeDtypeStruct((4, half), jnp.float32),
            jax.ShapeDtypeStruct((4, half), jnp.float32),
            jax.ShapeDtypeStruct((4, width), jnp.bfloat16),
        ),
        in_specs=[hbm] * (len(blocks) + 2) + [vmem] * len(rest),
        out_specs=(hbm, hbm, vmem, vmem, vmem),
        scratch_shapes=[
            pltpu.VMEM((feats, width), jnp.bfloat16),
            pltpu.VMEM((2 * half, feats), jnp.bfloat16),
            pltpu.VMEM((chunk, tile), jnp.float32),
            pltpu.VMEM((chunk, tile), jnp.float32),
            pltpu.VMEM((4, 2 * half, 128), jnp.float32),
            pltpu.VMEM((2 * half, 128), jnp.int32),
            pltpu.VMEM((2 * half, width), jnp.float32),
            pltpu.SemaphoreType.DMA((width // tile, len(blocks))),
            pltpu.SemaphoreType.DMA((2,)),
            pltpu.SemaphoreType.DMA((width // tile * (2 * half // chunk),)),
        ],
        compiler_params=pltpu.CompilerParams(vmem_limit_bytes=20 << 20),
        cost_estimate=pl.CostEstimate(
            flops=4 * half * width * feats, bytes_accessed=9 << 20, transcendentals=0
        ),
        name=f"scores{side}",
    )(*blocks, *units, *rest)


def unit_kernel(own_ref, beside_ref, *refs):
    out_ref = refs[-1]
    rows_n = out_ref.shape[0]
    yl = lax.axis_index("yl")
    x = lax.axis_index("x")
    for r in range(0, rows_n, 64):
        here = slice(r, r + 64)
        pieces = [(own_ref[here, :], 0, 0), (beside_ref[here, :], 1, 0)]
        for ref, dx in zip(refs, (3, 1, 2)):
            pieces += [(ref[k, here, :], k, dx) for k in range(2)]
        pieces = [(p.astype(jnp.float32), dy, dx) for p, dy, dx in pieces]
        total = sum(p * p for p, _, _ in pieces)
        scale = jnp.sqrt(jnp.sum(total, axis=1, keepdims=True) + EPS)
        for p, dy, dx in pieces:
            owner = lax.rem(yl + dy, 2) * 4 + lax.rem(x + dx, 4)
            cols = pl.ds(pl.multiple_of(owner * 128, 128), 128)
            out_ref[here, cols] = (p / scale).astype(jnp.bfloat16)


def unit_rows(own):
    beside = shifted(own, "yl", 2, 1)
    pair = jnp.stack([own, beside])
    parts = [own, beside] + [shifted(pair, "x", 4, k) for k in (1, 3, 2)]
    vmem = pl.BlockSpec(memory_space=pltpu.VMEM)
    return pl.pallas_call(
        unit_kernel,
        out_shape=jax.ShapeDtypeStruct((own.shape[0], 1024), jnp.bfloat16),
        in_specs=[vmem] * 5,
        out_specs=vmem,
        compiler_params=pltpu.CompilerParams(vmem_limit_bytes=8 << 20),
        name="unit",
    )(*parts)


def margin_kernel(kept0, kept1, got0, got1, row_ref, knn_own_ref, knn_got_ref, out_ref, ksrc):
    width = kept0.shape[1]
    core = lax.axis_index("core")

    @pl.when(pl.program_id(0) == 0)
    def _():
        a, b, c, d = (row_ref[i : i + 1, :] for i in range(4))
        mean = 0.25 * ((a + b) + (c + d))
        ksrc[...] = jnp.broadcast_to(mean, (128, mean.shape[1])).T

    rows_n = out_ref.shape[0]
    start = pl.multiple_of(pl.program_id(0) * rows_n, rows_n)
    own_place = core * (2 * width)
    got_place = (1 - core) * (2 * width)
    sides = (
        (kept0, knn_own_ref, 0, own_place),
        (kept1, knn_own_ref, width, own_place + width),
        (got0, knn_got_ref, 0, got_place),
        (got1, knn_got_ref, width, got_place + width),
    )
    for scores_ref, knn_ref, offset, place in sides:
        knn_tgt = knn_ref[:, offset : offset + width]
        cols = pl.ds(pl.multiple_of(place, width), width)
        for r in range(0, rows_n, 8):
            here = pl.ds(pl.multiple_of(start + r, 8), 8)
            x = scores_ref[r : r + 8, :]
            ratio = x / (0.5 * (ksrc[here, 0:1] + knn_tgt))
            out_ref[r : r + 8, cols] = jnp.where(x < -1.5, jnp.float32(0.0), ratio)


def margin(scores, row_list, knn_own, knn_got):
    rows_n, width = scores[0].shape
    block = 64
    vmem = pl.BlockSpec(memory_space=pltpu.VMEM)
    return pl.pallas_call(
        margin_kernel,
        grid=(rows_n // block,),
        out_shape=jax.ShapeDtypeStruct((rows_n, 4 * width), jnp.float32),
        in_specs=[pl.BlockSpec((block, width), lambda i: (i, 0))] * 4 + [vmem] * 3,
        out_specs=pl.BlockSpec((block, 4 * width), lambda i: (i, 0)),
        scratch_shapes=[pltpu.VMEM((rows_n, 128), jnp.float32)],
        compiler_params=pltpu.CompilerParams(
            dimension_semantics=("arbitrary",), vmem_limit_bytes=16 << 20
        ),
        name="margin",
    )(*scores, row_list, knn_own, knn_got)


def shifted(array, axis, size, by):
    return lax.ppermute(array, axis, [(i, (i + by) % size) for i in range(size)])


def from_everyone(array, axes, size):
    spread = jnp.broadcast_to(array[None], (size, *array.shape))
    return lax.all_to_all(spread, axes, 0, 0, tiled=True)


def up(array):
    return shifted(array, "z", 8, 1)


def down(array):
    return shifted(array, "z", 8, 7)


def across(array):
    return shifted(array, "yh", 2, 1)


def over(array):
    return shifted(array, "core", 2, 1)


PLACES = [(0, 0), (0, 1)] + [(dz, dy) for dz in (-1, 1, -2, 2, -3, 3, 4) for dy in (0, 1)]
BY_Y = (3, 4)


def gathered(own):
    a, b = {0: own}, {0: across(own)}
    for k in range(1, 5):
        a[-k] = up(a[1 - k])
        if k < 4:
            a[k] = down(a[k - 1])
            b[-k] = across(a[-k]) if k in BY_Y else up(b[1 - k])
            b[k] = across(a[k]) if k in BY_Y else down(b[k - 1])
    a[4] = a[-4]
    b[4] = across(a[4]) if 4 in BY_Y else down(b[3])
    return [(b if dy else a)[dz] for dz, dy in PLACES], b[0]


def body(src_emb, tgt_emb, src_ids, tgt_ids):
    core = lax.axis_index("core")
    first = core == 0
    own = tgt_emb.T
    half = own.shape[1] // 2
    mine = lax.dynamic_slice_in_dim(own, core * half, half, 1)
    theirs = over(lax.dynamic_slice_in_dim(own, (1 - core) * half, half, 1))
    chip = jnp.concatenate(
        [jnp.where(first, mine, theirs), jnp.where(first, theirs, mine)]
    )
    blocks, _ = gathered(chip)
    unit = unit_rows(src_emb)
    units = (unit, over(unit))
    sid = jnp.concatenate([src_ids, over(src_ids)])[None, :]
    tid = lax.dynamic_slice_in_dim(tgt_ids, core * half, half, 0)[None, :]

    quarter = half // 2
    kept0, sent0, row0, row0_pair, col0 = scores_and_lists(
        0, blocks, units, sid, tid[:, :quarter], ()
    )
    got0 = over(sent0)
    kept1, sent1, row1, row1_pair, col1 = scores_and_lists(
        1, blocks, units, sid, tid[:, quarter:], (row0, row0_pair)
    )
    col_lists = from_everyone(jnp.concatenate([col0, col1], axis=1), ("z", "yh"), 16)
    got1 = over(sent1)

    def joined(first, second):
        pairs = (
            merged(tuple(first[k : k + 4]), tuple(second[k : k + 4])) for k in (0, 4)
        )
        return jnp.stack([p for four in pairs for p in four])

    lists = jnp.concatenate([row1, row1_pair])
    lists = joined(lists, shifted(lists, "yl", 2, 1))
    lists = joined(lists, shifted(lists, "x", 4, 2))
    lists = joined(lists, shifted(lists, "x", 4, 1))
    col_lists = col_lists.astype(jnp.float32)
    a, b, c, d = merged_all([tuple(col_lists[k]) for k in range(16)])
    knn_own = 0.25 * ((a + b) + (c + d))
    swap = over(jnp.concatenate([lists[4:], knn_own.reshape(-1, lists.shape[1])]))
    row_list = jnp.stack(merged(tuple(lists[:4]), tuple(swap[:4])))
    knn_got = swap[4:].reshape(1, -1)
    return margin((kept0, kept1, got0, got1), row_list, knn_own[None, :], knn_got)


def solution(mesh):
    finer = Mesh(mesh.devices.reshape(8, 2, 2, 2, 4), ("z", "yh", "core", "yl", "x"))
    in_specs = (P(SRC, TGT), P(TGT, SRC), P(SRC), P(TGT))
    return jax.shard_map(
        body, mesh=finer, in_specs=in_specs, out_specs=P(SRC, TGT), check_vma=False
    )
```

```python
import functools

import jax
import jax.numpy as jnp
from jax import lax
from jax.experimental import pallas as pl
from jax.experimental.pallas import tpu as pltpu
from jax.sharding import Mesh
from jax.sharding import PartitionSpec as P

SRC = ("z", "yh", "core")
TGT = ("yl", "x")
EPS = 1e-06
EXCLUDED = -2.0


def bitonic_sorted(m):
    a, b, c, d = m
    a, c = jnp.maximum(a, c), jnp.minimum(a, c)
    b, d = jnp.maximum(b, d), jnp.minimum(b, d)
    a, b = jnp.maximum(a, b), jnp.minimum(a, b)
    c, d = jnp.maximum(c, d), jnp.minimum(c, d)
    return (a, b, c, d)


def top_half(first, second):
    return tuple(jnp.maximum(first[i], second[3 - i]) for i in range(4))


def merged(first, second):
    return bitonic_sorted(top_half(first, second))


def sorted_four(a, b, c, d):
    a, b = jnp.maximum(a, b), jnp.minimum(a, b)
    c, d = jnp.maximum(c, d), jnp.minimum(c, d)
    a, c = jnp.maximum(a, c), jnp.minimum(a, c)
    b, d = jnp.maximum(b, d), jnp.minimum(b, d)
    b, c = jnp.maximum(b, c), jnp.minimum(b, c)
    return (a, b, c, d)


def merged_all(lists):
    while len(lists) > 1:
        lists = [
            merged(lists[k], lists[k + 1]) if k + 1 < len(lists) else lists[k]
            for k in range(0, len(lists), 2)
        ]
    return lists[0]


def over_sublanes(lists):
    for shift in (4, 2, 1):
        lists = merged(lists, tuple(pltpu.roll(p, shift, 0) for p in lists))
    return lists


def score_kernel(n_blocks, side, *refs):
    blocks = refs[:n_blocks]
    unit_refs = refs[n_blocks : n_blocks + 2]
    sid_ref, tid_ref = refs[n_blocks + 2 : n_blocks + 4]
    refs = refs[n_blocks + 4 :]
    if side:
        row_before, refs = refs[:2], refs[2:]
    score_refs, row_refs, col_ref = refs[:2], refs[2:4], refs[4]
    tall, unit, even, odd, rows, sids, stage, tsem, usem, osem = refs[5:]
    feats, width = tall.shape
    rows_n = unit.shape[0]
    half = rows_n // 2
    chunk, tile = even.shape
    n_units = width // tile
    z = lax.axis_index("z")
    yh = lax.axis_index("yh")

    def copy(n, t):
        dz, dy = PLACES[n]
        owner = lax.rem(z + (8 + dz), 8) * 2 + lax.rem(yh + dy, 2)
        where = pl.ds(pl.multiple_of(owner * 64, 64), 64)
        offset = side * width if blocks[n].shape[1] > width else 0
        return pltpu.make_async_copy(
            blocks[n].at[:, pl.ds(offset + t * tile, tile)],
            tall.at[where, pl.ds(t * tile, tile)],
            tsem.at[t, n],
        )

    unit_copies = [
        pltpu.make_async_copy(
            unit_refs[k], unit.at[pl.ds(k * half, half), :], usem.at[k]
        )
        for k in range(2)
    ]
    for n in range(n_blocks):
        copy(n, 0).start()
    for c in unit_copies:
        c.start()
    for t in range(1, n_units):
        for n in range(n_blocks):
            copy(n, t).start()
    for r in range(0, rows_n, 128):
        ids = jnp.broadcast_to(sid_ref[:, r : r + 128], (128, 128))
        sids[r : r + 128, :] = ids.T
    for r in range(0, rows_n, 32):
        for i in range(4):
            rows[i, r : r + 32, :] = jnp.full((32, 128), EXCLUDED, jnp.float32)

    def columns(u):
        return slice(u * tile, u * tile + tile)

    def inverse_norm(u):
        total = jnp.zeros((8, tile), jnp.float32)
        for k in range(0, feats, 16):
            x = tall[k : k + 16, columns(u)].astype(jnp.float32)
            x = x * x
            total = total + (x[:8] + x[8:])
        return 1.0 / jnp.sqrt(jnp.sum(total, axis=0, keepdims=True) + EPS)

    sequence = [(u, r) for u in range(n_units) for r in range(0, rows_n, chunk)]
    buffers = (even, odd)

    def dot(k):
        u, r = sequence[k]
        buffers[k % 2][...] = jnp.dot(
            unit[r : r + chunk, :],
            tall[:, columns(u)],
            preferred_element_type=jnp.float32,
        )

    def sweep(u, r, dots, inside, inverse, tid, best):
        pieces = []
        for k in range(0, 32, 8):
            here = slice(r + k, r + k + 8)
            ids = sids[here, :]
            same = jnp.concatenate([ids] * (tile // 128), axis=1) == tid
            dotted = dots[inside + k : inside + k + 8, :] * inverse
            x = jnp.where(same, jnp.float32(EXCLUDED), dotted)
            pieces.append(x)
            kept = tuple(rows[i, here, :] for i in range(4))
            four = sorted_four(*(x[:, p : p + 128] for p in range(0, tile, 128)))
            kept = merged(kept, four)
            for i in range(4):
                rows[i, here, :] = kept[i]
        for k in range(0, 4, 2):
            here = slice(r + 8 * k, r + 8 * k + 16)
            both = jnp.concatenate(pieces[k : k + 2], axis=0)
            stage[here, columns(u)] = both.astype(stage.dtype)
        return merged(best, sorted_four(*pieces))

    def out_copy(k):
        u, r = sequence[k]
        cols = pl.ds(u * tile, tile)
        return pltpu.make_async_copy(
            stage.at[pl.ds(r, chunk), cols],
            score_refs[r // half].at[pl.ds(r % half, chunk), cols],
            osem.at[k],
        )

    for n in range(n_blocks):
        copy(n, 0).wait()
    for c in unit_copies:
        c.wait()
    dot(0)
    inverse = inverse_norm(0)
    best = (jnp.full((8, tile), EXCLUDED, jnp.float32),) * 4
    first = best
    for k, (u, r) in enumerate(sequence):
        if k + 1 < len(sequence):
            if sequence[k + 1][0] > u:
                for n in range(n_blocks):
                    copy(n, u + 1).wait()
                following = inverse_norm(u + 1)
            dot(k + 1)
        tid = tid_ref[:, columns(u)]
        for q in range(0, chunk, 32):
            best = sweep(u, r + q, buffers[k % 2], q, inverse, tid, best)
        out_copy(k).start()
        if r + chunk == rows_n:
            best = over_sublanes(best)
            for i in range(4):
                col_ref[i : i + 1, columns(u)] = best[i][0:1, :].astype(col_ref.dtype)
            if u + 1 < n_units:
                best, inverse = first, following

    for r in range(0, rows_n, 128):
        turned = [rows[i, r : r + 128, :].T for i in range(4)]
        lists = [
            tuple(turned[i][q : q + 8, :] for i in range(4)) for q in range(0, 128, 8)
        ]
        final = tuple(p[0:1, :] for p in over_sublanes(merged_all(lists)))
        here = slice(r % half, r % half + 128)
        if side:
            before = row_before[r // half]
            final = merged(final, tuple(before[i : i + 1, here] for i in range(4)))
        for i in range(4):
            row_refs[r // half][i : i + 1, here] = final[i]
    for k in range(len(sequence)):
        out_copy(k).wait()


def scores_and_lists(side, blocks, units, sid, tid, row_before):
    tile, chunk = 512, 256
    feats = 1024
    width = tid.shape[1]
    half = units[0].shape[0]
    vmem = pl.BlockSpec(memory_space=pltpu.VMEM)
    hbm = pl.BlockSpec(memory_space=pltpu.HBM)
    rest = [sid, tid, *row_before]
    return pl.pallas_call(
        functools.partial(score_kernel, len(blocks), side),
        out_shape=(
            pltpu.HBM((half, width), jnp.bfloat16),
            pltpu.HBM((half, width), jnp.bfloat16),
            jax.ShapeDtypeStruct((4, half), jnp.float32),
            jax.ShapeDtypeStruct((4, half), jnp.float32),
            jax.ShapeDtypeStruct((4, width), jnp.bfloat16),
        ),
        in_specs=[hbm] * (len(blocks) + 2) + [vmem] * len(rest),
        out_specs=(hbm, hbm, vmem, vmem, vmem),
        scratch_shapes=[
            pltpu.VMEM((feats, width), jnp.bfloat16),
            pltpu.VMEM((2 * half, feats), jnp.bfloat16),
            pltpu.VMEM((chunk, tile), jnp.float32),
            pltpu.VMEM((chunk, tile), jnp.float32),
            pltpu.VMEM((4, 2 * half, 128), jnp.float32),
            pltpu.VMEM((2 * half, 128), jnp.int32),
            pltpu.VMEM((2 * half, width), jnp.bfloat16),
            pltpu.SemaphoreType.DMA((width // tile, len(blocks))),
            pltpu.SemaphoreType.DMA((2,)),
            pltpu.SemaphoreType.DMA((width // tile * (2 * half // chunk),)),
        ],
        compiler_params=pltpu.CompilerParams(vmem_limit_bytes=20 << 20),
        cost_estimate=pl.CostEstimate(
            flops=4 * half * width * feats, bytes_accessed=9 << 20, transcendentals=0
        ),
        name=f"scores{side}",
    )(*blocks, *units, *rest)


def unit_kernel(src_ref, out_ref):
    rows_n = out_ref.shape[0]
    for r in range(0, rows_n, 64):
        pieces = [src_ref[j, r : r + 64, :].astype(jnp.float32) for j in range(8)]
        total = sum(x * x for x in pieces)
        scale = jnp.sqrt(jnp.sum(total, axis=1, keepdims=True) + EPS)
        for j in range(8):
            out_ref[r : r + 64, 128 * j : 128 * j + 128] = (pieces[j] / scale).astype(
                jnp.bfloat16
            )


def after(array, others):
    return lax.optimization_barrier((array, others))[0]


def unit_rows(src_all):
    vmem = pl.BlockSpec(memory_space=pltpu.VMEM)
    return pl.pallas_call(
        unit_kernel,
        out_shape=jax.ShapeDtypeStruct((src_all.shape[1], 1024), jnp.bfloat16),
        in_specs=[vmem],
        out_specs=vmem,
        compiler_params=pltpu.CompilerParams(vmem_limit_bytes=8 << 20),
        name="unit",
    )(src_all)


def margin_kernel(kept0, kept1, got0, got1, row_ref, knn_own_ref, knn_got_ref, out_ref, ksrc):
    width = kept0.shape[1]
    core = lax.axis_index("core")

    @pl.when(pl.program_id(0) == 0)
    def _():
        a, b, c, d = (row_ref[i : i + 1, :] for i in range(4))
        mean = 0.125 * ((a + b) + (c + d))
        ksrc[...] = jnp.broadcast_to(mean, (128, mean.shape[1])).T

    rows_n = out_ref.shape[0]
    start = pl.multiple_of(pl.program_id(0) * rows_n, rows_n)
    own_place = core * (2 * width)
    got_place = (1 - core) * (2 * width)
    sides = (
        (kept0, knn_own_ref, 0, own_place),
        (kept1, knn_own_ref, width, own_place + width),
        (got0, knn_got_ref, 0, got_place),
        (got1, knn_got_ref, width, got_place + width),
    )
    for scores_ref, knn_ref, offset, place in sides:
        knn_tgt = 0.125 * knn_ref[:, offset : offset + width]
        cols = pl.ds(pl.multiple_of(place, width), width)
        for r in range(0, rows_n, 16):
            here = pl.ds(pl.multiple_of(start + r, 16), 16)
            x = scores_ref[r : r + 16, :].astype(jnp.float32)
            ratio = x / (ksrc[here, 0:1] + knn_tgt)
            out_ref[r : r + 16, cols] = jnp.where(x < -1.5, jnp.float32(0.0), ratio)


def margin(scores, row_list, knn_own, knn_got):
    rows_n, width = scores[0].shape
    block = 64
    vmem = pl.BlockSpec(memory_space=pltpu.VMEM)
    return pl.pallas_call(
        margin_kernel,
        grid=(rows_n // block,),
        out_shape=jax.ShapeDtypeStruct((rows_n, 4 * width), jnp.float32),
        in_specs=[pl.BlockSpec((block, width), lambda i: (i, 0))] * 4 + [vmem] * 3,
        out_specs=pl.BlockSpec((block, 4 * width), lambda i: (i, 0)),
        scratch_shapes=[pltpu.VMEM((rows_n, 128), jnp.float32)],
        compiler_params=pltpu.CompilerParams(
            dimension_semantics=("arbitrary",), vmem_limit_bytes=16 << 20
        ),
        name="margin",
    )(*scores, row_list, knn_own, knn_got)


def shifted(array, axis, size, by):
    return lax.ppermute(array, axis, [(i, (i + by) % size) for i in range(size)])


def from_everyone(array, axes, size):
    spread = jnp.broadcast_to(array[None], (size, *array.shape))
    return lax.all_to_all(spread, axes, 0, 0, tiled=True)


def joined(arrays):
    if len(arrays) == 1:
        return arrays[0]
    groups = [
        merged_all([tuple(a[k : k + 4]) for a in arrays])
        for k in range(0, arrays[0].shape[0], 4)
    ]
    return jnp.stack([p for four in groups for p in four])


def up(array):
    return shifted(array, "z", 8, 1)


def down(array):
    return shifted(array, "z", 8, 7)


def across(array):
    return shifted(array, "yh", 2, 1)


def over(array):
    return shifted(array, "core", 2, 1)


PLACES = [(0, 0), (0, 1)] + [(dz, dy) for dz in (-1, 1, -2, 2, -3, 3, 4) for dy in (0, 1)]


def gathered(own, src_emb):
    a = {0: own, -1: up(own), 1: down(own)}
    a[2], a[-2] = down(a[1]), up(a[-1])
    b = {0: across(own)}
    src_all = from_everyone(src_emb, TGT, 8)
    a[2], a[-2], b[0], src_all = lax.optimization_barrier(
        (a[2], a[-2], b[0], src_all)
    )
    unit = unit_rows(src_all)
    a[3], a[-3] = down(a[2]), up(a[-2])
    a[4] = up(a[-3])
    for k in range(1, 4):
        b[k], b[-k] = down(b[k - 1]), up(b[1 - k])
    b[4] = down(b[3])
    return [(b if dy else a)[dz] for dz, dy in PLACES], unit


def body(src_emb, tgt_emb, src_ids, tgt_ids):
    core = lax.axis_index("core")
    first = core == 0
    own = tgt_emb.T
    half = own.shape[1] // 2
    mine = lax.dynamic_slice_in_dim(own, core * half, half, 1)
    theirs = over(lax.dynamic_slice_in_dim(own, (1 - core) * half, half, 1))
    chip = jnp.concatenate(
        [jnp.where(first, mine, theirs), jnp.where(first, theirs, mine)]
    )
    blocks, unit = gathered(chip, src_emb)
    units = (unit, over(unit))
    sid = jnp.concatenate([src_ids, over(src_ids)])[None, :]
    tid = lax.dynamic_slice_in_dim(tgt_ids, core * half, half, 0)[None, :]

    quarter = half // 2
    kept0, sent0, row0, row0_pair, col0 = scores_and_lists(
        0, blocks, units, sid, tid[:, :quarter], ()
    )
    got0 = over(sent0)
    kept1, sent1, row1, row1_pair, col1 = scores_and_lists(
        1, blocks, units, sid, tid[:, quarter:], (row0, row0_pair)
    )
    got1 = over(sent1)
    cols = jnp.concatenate([col0, col1], axis=1)
    rows = jnp.concatenate([row1, row1_pair])
    rows = joined([rows, shifted(rows, "yl", 2, 1)])
    cols = joined([cols, across(cols)])
    spread = jnp.broadcast_to(cols[None], (8, *cols.shape))
    far = lax.all_to_all(spread, "z", 0, 0, tiled=True)
    rows = after(rows, spread)
    rows = joined([rows] + [shifted(rows, "x", 4, k) for k in (1, 2, 3)])
    row_list = joined([rows[:4], over(rows[4:])])
    far = far.astype(jnp.float32)
    a, b, c, d = merged_all([tuple(far[k]) for k in range(8)])
    knn_own = ((a + b) + (c + d))[None, :]
    return margin((kept0, kept1, got0, got1), row_list, knn_own, over(knn_own))


def solution(mesh):
    finer = Mesh(mesh.devices.reshape(8, 2, 2, 2, 4), ("z", "yh", "core", "yl", "x"))
    in_specs = (P(SRC, TGT), P(TGT, SRC), P(SRC), P(TGT))
    return jax.shard_map(
        body, mesh=finer, in_specs=in_specs, out_specs=P(SRC, TGT), check_vma=False
    )
```

```python
import functools

import jax
import jax.numpy as jnp
from jax import lax
from jax.experimental import pallas as pl
from jax.experimental.pallas import tpu as pltpu
from jax.sharding import Mesh
from jax.sharding import PartitionSpec as P

SRC = ("z", "yh", "core")
TGT = ("yl", "x")
EPS = 1e-06
EXCLUDED = -2.0


def bitonic_sorted(m):
    a, b, c, d = m
    a, c = jnp.maximum(a, c), jnp.minimum(a, c)
    b, d = jnp.maximum(b, d), jnp.minimum(b, d)
    a, b = jnp.maximum(a, b), jnp.minimum(a, b)
    c, d = jnp.maximum(c, d), jnp.minimum(c, d)
    return (a, b, c, d)


def top_half(first, second):
    return tuple(jnp.maximum(first[i], second[3 - i]) for i in range(4))


def merged(first, second):
    return bitonic_sorted(top_half(first, second))


def sorted_four(a, b, c, d):
    a, b = jnp.maximum(a, b), jnp.minimum(a, b)
    c, d = jnp.maximum(c, d), jnp.minimum(c, d)
    a, c = jnp.maximum(a, c), jnp.minimum(a, c)
    b, d = jnp.maximum(b, d), jnp.minimum(b, d)
    b, c = jnp.maximum(b, c), jnp.minimum(b, c)
    return (a, b, c, d)


def merged_all(lists):
    while len(lists) > 1:
        lists = [
            merged(lists[k], lists[k + 1]) if k + 1 < len(lists) else lists[k]
            for k in range(0, len(lists), 2)
        ]
    return lists[0]


def over_sublanes(lists):
    for shift in (4, 2, 1):
        lists = merged(lists, tuple(pltpu.roll(p, shift, 0) for p in lists))
    return lists


def score_kernel(n_blocks, *refs):
    blocks = refs[:n_blocks]
    unit_refs = refs[n_blocks : n_blocks + 2]
    sid_ref, tid_ref = refs[n_blocks + 2 : n_blocks + 4]
    refs = refs[n_blocks + 4 :]
    score_refs, row_refs, col_ref = refs[:2], refs[2:4], refs[4]
    tall, unit, even, odd, rows, sids, stage, tsem, usem, osem = refs[5:]
    feats, width = tall.shape
    rows_n = unit.shape[0]
    half = rows_n // 2
    chunk, tile = even.shape
    n_units = width // tile
    z = lax.axis_index("z")
    yh = lax.axis_index("yh")

    def copy(n, t):
        dz, dy = PLACES[n]
        owner = lax.rem(z + (8 + dz), 8) * 2 + lax.rem(yh + dy, 2)
        where = pl.ds(pl.multiple_of(owner * 64, 64), 64)
        return pltpu.make_async_copy(
            blocks[n].at[:, pl.ds(t * tile, tile)],
            tall.at[where, pl.ds(t * tile, tile)],
            tsem.at[t, n],
        )

    unit_copies = [
        pltpu.make_async_copy(
            unit_refs[k], unit.at[pl.ds(k * half, half), :], usem.at[k]
        )
        for k in range(2)
    ]
    for n in range(n_blocks):
        copy(n, 0).start()
    for c in unit_copies:
        c.start()
    for t in range(1, n_units):
        for n in range(n_blocks):
            copy(n, t).start()
    for r in range(0, rows_n, 128):
        ids = jnp.broadcast_to(sid_ref[:, r : r + 128], (128, 128))
        sids[r : r + 128, :] = ids.T
    for r in range(0, rows_n, 32):
        for i in range(4):
            rows[i, r : r + 32, :] = jnp.full((32, 128), EXCLUDED, jnp.float32)

    def columns(u):
        return slice(u * tile, u * tile + tile)

    def inverse_norm(u):
        total = jnp.zeros((8, tile), jnp.float32)
        for k in range(0, feats, 16):
            x = tall[k : k + 16, columns(u)].astype(jnp.float32)
            x = x * x
            total = total + (x[:8] + x[8:])
        return 1.0 / jnp.sqrt(jnp.sum(total, axis=0, keepdims=True) + EPS)

    sequence = [(u, r) for u in range(n_units) for r in range(0, rows_n, chunk)]
    buffers = (even, odd)

    def dot(k):
        u, r = sequence[k]
        buffers[k % 2][...] = jnp.dot(
            unit[r : r + chunk, :],
            tall[:, columns(u)],
            preferred_element_type=jnp.float32,
        )

    def sweep(u, r, dots, inside, inverse, tid, best):
        pieces = []
        for k in range(0, 32, 8):
            here = slice(r + k, r + k + 8)
            ids = sids[here, :]
            same = jnp.concatenate([ids] * (tile // 128), axis=1) == tid
            dotted = dots[inside + k : inside + k + 8, :] * inverse
            x = jnp.where(same, jnp.float32(EXCLUDED), dotted)
            pieces.append(x)
            kept = tuple(rows[i, here, :] for i in range(4))
            four = sorted_four(*(x[:, p : p + 128] for p in range(0, tile, 128)))
            kept = merged(kept, four)
            for i in range(4):
                rows[i, here, :] = kept[i]
        for k in range(0, 4, 2):
            here = slice(r + 8 * k, r + 8 * k + 16)
            both = jnp.concatenate(pieces[k : k + 2], axis=0)
            stage[here, columns(u)] = both.astype(stage.dtype)
        return merged(best, sorted_four(*pieces))

    def out_copy(k):
        u, r = sequence[k]
        cols = pl.ds(u * tile, tile)
        return pltpu.make_async_copy(
            stage.at[pl.ds(r, chunk), cols],
            score_refs[r // half].at[pl.ds(r % half, chunk), cols],
            osem.at[k],
        )

    for n in range(n_blocks):
        copy(n, 0).wait()
    for c in unit_copies:
        c.wait()
    dot(0)
    inverse = inverse_norm(0)
    best = (jnp.full((8, tile), EXCLUDED, jnp.float32),) * 4
    first = best
    for k, (u, r) in enumerate(sequence):
        if k + 1 < len(sequence):
            if sequence[k + 1][0] > u:
                for n in range(n_blocks):
                    copy(n, u + 1).wait()
                following = inverse_norm(u + 1)
            dot(k + 1)
        tid = tid_ref[:, columns(u)]
        for q in range(0, chunk, 32):
            best = sweep(u, r + q, buffers[k % 2], q, inverse, tid, best)
        out_copy(k).start()
        if r + chunk == rows_n:
            best = over_sublanes(best)
            for i in range(4):
                col_ref[i : i + 1, columns(u)] = best[i][0:1, :].astype(col_ref.dtype)
            if u + 1 < n_units:
                best, inverse = first, following

    for r in range(0, rows_n, 128):
        turned = [rows[i, r : r + 128, :].T for i in range(4)]
        lists = [
            tuple(turned[i][q : q + 8, :] for i in range(4)) for q in range(0, 128, 8)
        ]
        final = tuple(p[0:1, :] for p in over_sublanes(merged_all(lists)))
        here = slice(r % half, r % half + 128)
        for i in range(4):
            row_refs[r // half][i : i + 1, here] = final[i]
    for k in range(len(sequence)):
        out_copy(k).wait()


def scores_and_lists(blocks, units, sid, tid):
    tile, chunk = 512, 256
    feats = 1024
    width = tid.shape[1]
    half = units[0].shape[0]
    vmem = pl.BlockSpec(memory_space=pltpu.VMEM)
    hbm = pl.BlockSpec(memory_space=pltpu.HBM)
    rest = [sid, tid]
    return pl.pallas_call(
        functools.partial(score_kernel, len(blocks)),
        out_shape=(
            pltpu.HBM((half, width), jnp.bfloat16),
            pltpu.HBM((half, width), jnp.bfloat16),
            jax.ShapeDtypeStruct((4, half), jnp.float32),
            jax.ShapeDtypeStruct((4, half), jnp.float32),
            jax.ShapeDtypeStruct((4, width), jnp.bfloat16),
        ),
        in_specs=[hbm] * (len(blocks) + 2) + [vmem] * len(rest),
        out_specs=(hbm, hbm, vmem, vmem, vmem),
        scratch_shapes=[
            pltpu.VMEM((feats, width), jnp.bfloat16),
            pltpu.VMEM((2 * half, feats), jnp.bfloat16),
            pltpu.VMEM((chunk, tile), jnp.float32),
            pltpu.VMEM((chunk, tile), jnp.float32),
            pltpu.VMEM((4, 2 * half, 128), jnp.float32),
            pltpu.VMEM((2 * half, 128), jnp.int32),
            pltpu.VMEM((2 * half, width), jnp.bfloat16),
            pltpu.SemaphoreType.DMA((width // tile, len(blocks))),
            pltpu.SemaphoreType.DMA((2,)),
            pltpu.SemaphoreType.DMA((width // tile * (2 * half // chunk),)),
        ],
        compiler_params=pltpu.CompilerParams(vmem_limit_bytes=24 << 20),
        cost_estimate=pl.CostEstimate(
            flops=4 * half * width * feats, bytes_accessed=12 << 20, transcendentals=0
        ),
        name="scores",
    )(*blocks, *units, *rest)


def unit_kernel(src_ref, out_ref):
    rows_n = out_ref.shape[0]
    yl = lax.axis_index("yl")
    for r in range(0, rows_n, 64):
        here = slice(r, r + 64)
        pieces = [
            (x, k, src_ref[x, k, here, :].astype(jnp.float32))
            for x in range(4)
            for k in range(2)
        ]
        total = sum(p * p for _, _, p in pieces)
        scale = jnp.sqrt(jnp.sum(total, axis=1, keepdims=True) + EPS)
        for x, k, p in pieces:
            owner = lax.rem(yl + k, 2) * 4 + x
            cols = pl.ds(pl.multiple_of(owner * 128, 128), 128)
            out_ref[here, cols] = (p / scale).astype(jnp.bfloat16)


def after(array, others):
    return lax.optimization_barrier((array, others))[0]


def unit_rows(src_all):
    vmem = pl.BlockSpec(memory_space=pltpu.VMEM)
    return pl.pallas_call(
        unit_kernel,
        out_shape=jax.ShapeDtypeStruct((src_all.shape[2], 1024), jnp.bfloat16),
        in_specs=[vmem],
        out_specs=vmem,
        compiler_params=pltpu.CompilerParams(vmem_limit_bytes=8 << 20),
        name="unit",
    )(src_all)


def margin_kernel(kept_ref, got_ref, row_ref, knn_own_ref, knn_got_ref, out_ref, ksrc):
    width = kept_ref.shape[1]
    core = lax.axis_index("core")

    @pl.when(pl.program_id(0) == 0)
    def _():
        a, b, c, d = (row_ref[i : i + 1, :] for i in range(4))
        mean = 0.125 * ((a + b) + (c + d))
        ksrc[...] = jnp.broadcast_to(mean, (128, mean.shape[1])).T

    rows_n = out_ref.shape[0]
    start = pl.multiple_of(pl.program_id(0) * rows_n, rows_n)
    sides = (
        (kept_ref, knn_own_ref, core * width),
        (got_ref, knn_got_ref, (1 - core) * width),
    )
    for scores_ref, knn_ref, place in sides:
        knn_tgt = 0.125 * knn_ref[...]
        cols = pl.ds(pl.multiple_of(place, width), width)
        for r in range(0, rows_n, 16):
            here = pl.ds(pl.multiple_of(start + r, 16), 16)
            x = scores_ref[r : r + 16, :].astype(jnp.float32)
            ratio = x / (ksrc[here, 0:1] + knn_tgt)
            out_ref[r : r + 16, cols] = jnp.where(x < -1.5, jnp.float32(0.0), ratio)


def margin(kept, got, row_list, knn_own, knn_got):
    rows_n, width = kept.shape
    block = 64
    vmem = pl.BlockSpec(memory_space=pltpu.VMEM)
    return pl.pallas_call(
        margin_kernel,
        grid=(rows_n // block,),
        out_shape=jax.ShapeDtypeStruct((rows_n, 2 * width), jnp.float32),
        in_specs=[pl.BlockSpec((block, width), lambda i: (i, 0))] * 2 + [vmem] * 3,
        out_specs=pl.BlockSpec((block, 2 * width), lambda i: (i, 0)),
        scratch_shapes=[pltpu.VMEM((rows_n, 128), jnp.float32)],
        compiler_params=pltpu.CompilerParams(
            dimension_semantics=("arbitrary",), vmem_limit_bytes=16 << 20
        ),
        name="margin",
    )(kept, got, row_list, knn_own, knn_got)


def shifted(array, axis, size, by):
    return lax.ppermute(array, axis, [(i, (i + by) % size) for i in range(size)])


def from_everyone(array, axes, size):
    spread = jnp.broadcast_to(array[None], (size, *array.shape))
    return lax.all_to_all(spread, axes, 0, 0, tiled=True)


def joined(arrays):
    if len(arrays) == 1:
        return arrays[0]
    groups = [
        merged_all([tuple(a[k : k + 4]) for a in arrays])
        for k in range(0, arrays[0].shape[0], 4)
    ]
    return jnp.stack([p for four in groups for p in four])


def up(array):
    return shifted(array, "z", 8, 1)


def down(array):
    return shifted(array, "z", 8, 7)


def across(array):
    return shifted(array, "yh", 2, 1)


def over(array):
    return shifted(array, "core", 2, 1)


PLACES = [(0, 0), (0, 1)] + [(dz, dy) for dz in (-1, 1, -2, 2, -3, 3, 4) for dy in (0, 1)]


def gathered(own, src_emb):
    a = {0: own, -1: up(own), 1: down(own)}
    a[2], a[-2] = down(a[1]), up(a[-1])
    b = {0: across(own)}
    beside = shifted(src_emb, "yl", 2, 1)
    src_all = from_everyone(jnp.stack([src_emb, beside]), "x", 4)
    a[3], a[-3] = down(a[2]), up(a[-2])
    b[1], b[-1] = down(b[0]), up(b[0])
    a[3], a[-3], b[1], b[-1], src_all = lax.optimization_barrier(
        (a[3], a[-3], b[1], b[-1], src_all)
    )
    unit = unit_rows(src_all)
    a[4] = up(a[-3])
    b[2], b[-2] = down(b[1]), up(b[-1])
    b[3], b[-3] = down(b[2]), across(a[-3])
    b[4] = across(a[4])
    return [(b if dy else a)[dz] for dz, dy in PLACES], unit


def body(src_emb, tgt_emb, src_ids, tgt_ids):
    core = lax.axis_index("core")
    first = core == 0
    own = tgt_emb.T
    half = own.shape[1] // 2
    mine = lax.dynamic_slice_in_dim(own, core * half, half, 1)
    theirs = over(lax.dynamic_slice_in_dim(own, (1 - core) * half, half, 1))
    chip = jnp.concatenate(
        [jnp.where(first, mine, theirs), jnp.where(first, theirs, mine)]
    )
    blocks, unit = gathered(chip, src_emb)
    units = (unit, over(unit))
    sid = jnp.concatenate([src_ids, over(src_ids)])[None, :]
    tid = lax.dynamic_slice_in_dim(tgt_ids, core * half, half, 0)[None, :]

    kept, sent, rows, rows_pair, cols = scores_and_lists(blocks, units, sid, tid)
    got = over(sent)
    rows = jnp.concatenate([rows, rows_pair])
    rows = joined([rows, shifted(rows, "yl", 2, 1)])
    cols = joined([cols, across(cols)])
    spread = jnp.broadcast_to(cols[None], (8, *cols.shape))
    far = lax.all_to_all(spread, "z", 0, 0, tiled=True)
    rows = after(rows, spread)
    rows = joined([rows] + [shifted(rows, "x", 4, k) for k in (1, 2, 3)])
    row_list = joined([rows[:4], over(rows[4:])])
    far = far.astype(jnp.float32)
    a, b, c, d = merged_all([tuple(far[k]) for k in range(8)])
    knn_own = ((a + b) + (c + d))[None, :]
    return margin(kept, got, row_list, knn_own, over(knn_own))


def solution(mesh):
    finer = Mesh(mesh.devices.reshape(8, 2, 2, 2, 4), ("z", "yh", "core", "yl", "x"))
    in_specs = (P(SRC, TGT), P(TGT, SRC), P(SRC), P(TGT))
    return jax.shard_map(
        body, mesh=finer, in_specs=in_specs, out_specs=P(SRC, TGT), check_vma=False
    )
```
